32 devices in a mesh: groups: 2 (over y), ctx: 4 (over z), kvh: 2 (over x), rep: 2 (over core).
Axes of the slice: x: 2, y: 2, z: 4, core: 2. Of those that a mesh axis runs over, the one named last changes fastest.
Arguments:
- context_queries: bfloat16 [8192, 8192], P(('groups', 'ctx'), ('kvh', 'rep')), parts along dimension 0, may hold values from -128 to 128
- context_keys: bfloat16 [8192, 1024], P(('groups', 'ctx'), 'kvh'), parts along dimension 0, may hold values from -4 to 4
- context_values: bfloat16 [8192, 1024], P(('groups', 'ctx'), 'kvh'), parts along dimension 0, may hold values from -16 to 16
- query_queries: bfloat16 [128, 8192], P(('groups', 'ctx'), ('kvh', 'rep')), parts along dimension 0, may hold values from -128 to 128
- query_keys: bfloat16 [128, 1024], P(('groups', 'ctx'), 'kvh'), parts along dimension 0, may hold values from -4 to 4
- query_values: bfloat16 [128, 1024], P(('groups', 'ctx'), 'kvh'), parts along dimension 0, may hold values from -4 to 4
Outputs:
- context_out: bfloat16 [8192, 8192], P(('groups', 'ctx'), ('kvh', 'rep')), parts along dimension 0
- query_out: bfloat16 [128, 8192], P(('groups', 'ctx'), ('kvh', 'rep')), parts along dimension 0
The draws below stay inside these ranges and needn't reach their ends.
There are 2 independent parts, one for each index of `groups`. The reference program is written for one: setup_inputs(seed, part) draws one part's arguments, and reference() takes and returns one part's arrays. A program takes and returns all parts, laid end to end along the dimension named above; each array names one. Nothing has to cross between parts.
All inputs are finite; a program needn't handle non-finite values.
Results may differ from the reference program's by a relative error of at most 0.0026.
Values may be sent and summed in bfloat16 or wider, within the bound.
No kernel may reach another device: no remote copies, remote signals or barrier semaphores. Data moves between devices by JAX's collectives and lax.ppermute only.
A program may use at most 192 MiB of HBM per device.

```python
import math
import jax
import jax.numpy as jnp
from jax import lax

H = 64
KVH = 8
HD = 128
BLK = 1024
QSH = 16
BLOCKS = 4
CTX = 4096
QN = 64


BROAD = 32.0


def base_keys(key):
    keys_all = jnp.clip(jax.random.normal(jax.random.fold_in(key, 11), (CTX, KVH * HD), jnp.float32), -4.0, 4.0)
    return keys_all


def sign_rows(key, shape):
    return jnp.where(jax.random.bernoulli(key, 0.5, shape), 1.0, -1.0).astype(jnp.float32)


def draw_context_keys(key, part):
    return base_keys(key).astype(jnp.bfloat16)


def draw_context_queries(key, part):
    queries = jnp.clip(jax.random.normal(jax.random.fold_in(key, 12), (CTX, H * HD), jnp.float32), -4.0, 4.0)
    blocks = queries.reshape(BLOCKS, BLK, H * HD)
    broad_rows = BROAD * sign_rows(jax.random.fold_in(key, 16), (BLOCKS, 2, H * HD))
    blocks = blocks.at[:, BLK // 4:BLK // 4 + 2].set(broad_rows)
    queries = blocks.reshape(CTX, H * HD)
    return queries.astype(jnp.bfloat16)


def draw_query_queries(key, part):
    queries = jnp.clip(jax.random.normal(jax.random.fold_in(key, 14), (QN, H * HD), jnp.float32), -4.0, 4.0)
    queries = queries.at[0:2].set(BROAD * sign_rows(jax.random.fold_in(key, 17), (2, H * HD)))
    return queries.astype(jnp.bfloat16)


def draw_context_values(key, part):
    offsets = 2.0 * jnp.clip(jax.random.normal(jax.random.fold_in(key, 13), (BLOCKS, KVH * HD), jnp.float32), -3.0, 3.0)
    noise = jnp.clip(jax.random.normal(jax.random.fold_in(key, 15), (CTX, KVH * HD), jnp.float32), -3.5, 3.5)
    return (jnp.repeat(offsets, BLK, axis=0) + noise + 1.5 * base_keys(key)).astype(jnp.bfloat16)


def levels(key, extent, cuts, least, largest):
    def one(axis_at, parts):
        steps = jax.random.uniform(jax.random.fold_in(jax.random.fold_in(key, 6), axis_at), (parts,), jnp.float32, least / len(cuts), largest / len(cuts))
        return jnp.repeat(jnp.exp(steps), extent[axis_at] // parts).reshape((-1,) + (1,) * (len(extent) - axis_at - 1))

    loudness = one(*cuts[0])
    for cut in cuts[1:]:
        loudness = loudness * one(*cut)
    return loudness


def scatter_about(own_key, extent, scale, bound, split=(), kind=jnp.bfloat16):
    entries = scale * jax.random.normal(own_key, extent, jnp.float32)
    if split:
        entries = entries * levels(own_key, extent, split, -0.22, 0.18)
    return jnp.clip(entries, -bound, bound).astype(kind)


def setup_inputs(seed: int = 0, part: int = 0) -> dict:
    splits = jax.random.split(jax.random.key(seed), 7)
    part_splits = jax.random.split(jax.random.fold_in(splits[6], part), 7)
    return {
        "context_queries": draw_context_queries(jax.random.fold_in(jax.random.fold_in(splits[6], part), 71), part),
        "context_keys": draw_context_keys(jax.random.fold_in(jax.random.fold_in(splits[6], part), 71), part),
        "context_values": draw_context_values(jax.random.fold_in(jax.random.fold_in(splits[6], part), 71), part),
        "query_queries": draw_query_queries(jax.random.fold_in(jax.random.fold_in(splits[6], part), 71), part),
        "query_keys": scatter_about(part_splits[4], (QN, KVH * HD), 1.0, 4.0, ((0, 4), (1, 2))),
        "query_values": scatter_about(part_splits[5], (QN, KVH * HD), 1.0, 4.0, ((0, 4), (1, 2))),
    }


MASKED = -1e+30

def reference(context_queries, context_keys, context_values, query_queries, query_keys, query_values):
    group_size = H // KVH
    scaling = 1.0 / math.sqrt(HD)
    query_blocks = context_queries.astype(jnp.float32).reshape(BLOCKS, BLK, KVH, group_size, HD)
    key_blocks = context_keys.astype(jnp.float32).reshape(BLOCKS, BLK, KVH, HD)
    value_blocks = context_values.astype(jnp.float32).reshape(BLOCKS, BLK, KVH, HD)
    positions = jnp.arange(BLK, dtype=jnp.int32)
    causal = positions[None, :] <= positions[:, None]

    def phase_one(element):
        block_queries, block_keys, block_values, block_index = element
        key_rows = jnp.concatenate([key_blocks[0], block_keys], 0)
        value_rows = jnp.concatenate([value_blocks[0], block_values], 0)
        scores = jnp.einsum('qkgd,pkd->kgqp', block_queries, key_rows) * scaling
        visible = jnp.concatenate([jnp.broadcast_to(block_index > 0, (BLK, BLK)), causal], 1)
        scores = jnp.where(visible, scores, MASKED)
        maxima = lax.optimization_barrier(jnp.max(scores, axis=-1, keepdims=True))
        weights = jnp.exp(scores - maxima)
        totals = lax.optimization_barrier(jnp.sum(weights, axis=-1))
        rounded = lax.optimization_barrier(weights.astype(jnp.bfloat16)).astype(jnp.float32)
        result = jnp.einsum('kgqp,pkd->qkgd', rounded, value_rows)
        result = result / jnp.transpose(totals, (2, 0, 1))[..., None]
        return result.reshape(BLK, H * HD).astype(jnp.bfloat16)
    context_out = lax.map(phase_one, (query_blocks, key_blocks, value_blocks, jnp.arange(BLOCKS, dtype=jnp.int32)))
    context_out = context_out.reshape(CTX, H * HD)
    final_queries = query_queries.astype(jnp.float32).reshape(QN, KVH, group_size, HD)
    final_keys = query_keys.astype(jnp.float32).reshape(BLOCKS, QSH, KVH, HD)
    final_values = query_values.astype(jnp.float32).reshape(BLOCKS, QSH, KVH, HD)
    query_pos = jnp.arange(QN, dtype=jnp.int32)

    def phase_two(element):
        block_keys, block_values, extra_keys, extra_values, block_index = element
        key_rows = jnp.concatenate([block_keys, extra_keys], 0)
        value_rows = jnp.concatenate([block_values, extra_values], 0)
        scores = jnp.einsum('rkgd,pkd->kgrp', final_queries, key_rows) * scaling
        own_rows = block_index * QSH + jnp.arange(QSH, dtype=jnp.int32)
        visible = jnp.concatenate([jnp.ones((QN, BLK), dtype=bool), own_rows[None, :] <= query_pos[:, None]], 1)
        scores = jnp.where(visible, scores, MASKED)
        maxima = lax.optimization_barrier(jnp.max(scores, axis=-1))
        weights = jnp.exp(scores - maxima[..., None])
        totals = lax.optimization_barrier(jnp.sum(weights, axis=-1))
        rounded = lax.optimization_barrier(weights.astype(jnp.bfloat16)).astype(jnp.float32)
        result = jnp.einsum('kgrp,pkd->kgrd', rounded, value_rows)
        return (maxima, totals, result)
    maxima_all, totals_all, outputs_all = lax.map(phase_two, (key_blocks, value_blocks, final_keys, final_values, jnp.arange(BLOCKS, dtype=jnp.int32)))
    overall = lax.optimization_barrier(jnp.max(maxima_all, axis=0))
    factor = jnp.exp(maxima_all - overall[None])
    summed = lax.optimization_barrier(jnp.sum(factor * totals_all, axis=0))
    numerator = lax.optimization_barrier(jnp.sum(factor[..., None] * outputs_all, axis=0))
    query_out = (numerator / summed[..., None]).transpose(2, 0, 1, 3).reshape(QN, H * HD).astype(jnp.bfloat16)
    return (context_out, query_out)
```

```python
import functools
import math

import jax
import jax.numpy as jnp
from jax import lax
from jax.experimental import pallas as pl
from jax.experimental.pallas import tpu as pltpu
from jax.sharding import PartitionSpec as P

HD = 128
MASKED = -1e30
SCALE = math.log2(math.e) / math.sqrt(HD)
SAFE = 2.0**100
F32 = jnp.float32
BF16 = jnp.bfloat16
NT = (((1,), (1,)), ((), ()))
NN = (((1,), (0,)), ((), ()))
VMEM_LIMIT = 56 * 2**20


def dot(a, b, dims):
    return lax.dot_general(a, b, dims, preferred_element_type=F32)


def tile_of(length):
    return math.gcd(length, 256)


def own_kernel(off_ref, q_ref, k_ref, v_ref, acc_ref, stat_ref, *, heads):
    rows = q_ref.shape[0]
    tile = tile_of(rows)
    values = v_ref[...].T
    jobs = [(h, i) for h in range(heads) for i in range(rows // tile)]
    causal = lax.broadcasted_iota(jnp.int32, (tile, tile), 0) <= lax.broadcasted_iota(
        jnp.int32, (tile, tile), 1
    )

    def score(job):
        h, i = job
        q = q_ref[i * tile : (i + 1) * tile, h * HD : (h + 1) * HD]
        s = dot(k_ref[: (i + 1) * tile, :], q, NT)
        last = jnp.where(causal, s[i * tile :], MASKED)
        return last if i == 0 else jnp.concatenate([s[: i * tile], last], 0)

    def soften(s):
        top = jnp.max(s, 0, keepdims=True) * SCALE
        p = jnp.exp2(s * SCALE - top)
        return p.astype(BF16), top, jnp.sum(p, 0, keepdims=True)

    def finish(job, state):
        h, i = job
        p, top, total = state
        columns = slice(i * tile, (i + 1) * tile)
        acc_ref[h, :, columns] = dot(values[:, : (i + 1) * tile], p, NN)
        stat_ref[h, 0:1, columns] = top
        stat_ref[h, 1:2, columns] = total

    scores, weights = {0: score(jobs[0])}, {}
    for t in range(len(jobs) + 1):
        if t + 1 < len(jobs):
            scores[t + 1] = score(jobs[t + 1])
        if t < len(jobs):
            weights[t] = soften(scores.pop(t))
        if t > 0:
            finish(jobs[t - 1], weights.pop(t - 1))


def anchor_kernel(pos_ref, q_ref, acc_ref, stat_ref, *refs, heads, parts):
    part_refs, (o_ref, k_ref, vt_ref) = refs[:parts], refs[-3:]
    rows = q_ref.shape[0]
    tile = tile_of(rows)
    size = part_refs[0].shape[1]
    jobs = [(h, i) for h in range(heads) for i in range(rows // tile)]

    def query(h, i):
        return q_ref[i * tile : (i + 1) * tile, h * HD : (h + 1) * HD]

    @pl.when(pos_ref[0] == 0)
    def _():
        for h, i in jobs:
            columns = slice(i * tile, (i + 1) * tile)
            out = acc_ref[h, :, columns] / stat_ref[h, 1:2, columns]
            o_ref[columns, h * HD : (h + 1) * HD] = out.T.astype(BF16)

    @pl.when(pos_ref[0] > 0)
    def _():
        @pl.when(pl.program_id(0) == 0)
        def _():
            def assemble(v_ref):
                for r in range(parts):
                    start = pl.multiple_of(pos_ref[1 + r], 16)
                    k_ref[pl.ds(start, size), :] = part_refs[r][0]
                    v_ref[pl.ds(start, size), :] = part_refs[r][1]
                vt_ref[...] = v_ref[...].T

            pl.run_scoped(assemble, pltpu.VMEM(k_ref.shape, BF16))

        largest = None
        for h, i in jobs:
            columns = slice(i * tile, (i + 1) * tile)
            s = dot(k_ref[...], query(h, i), NT)
            p = jnp.exp2(s * SCALE - stat_ref[h, 0:1, columns])
            total = stat_ref[h, 1:2, columns] + jnp.sum(p, 0, keepdims=True)
            out = acc_ref[h, :, columns] + dot(vt_ref[...], p.astype(BF16), NN)
            o_ref[columns, h * HD : (h + 1) * HD] = (out / total).T.astype(BF16)
            worst = jnp.where(total < SAFE, 0.0, 1.0)
            largest = worst if largest is None else jnp.maximum(largest, worst)

        @pl.when(jnp.max(largest) > 0.0)
        def _():
            for h in range(heads):

                @pl.loop(0, rows // tile)
                def _(i):
                    columns = pl.ds(pl.multiple_of(i * tile, tile), tile)
                    s = dot(k_ref[...], q_ref[columns, h * HD : (h + 1) * HD], NT) * SCALE
                    own_top = stat_ref[h, 0:1, columns]
                    top = jnp.maximum(own_top, jnp.max(s, 0, keepdims=True))
                    p = jnp.exp2(s - top)
                    factor = jnp.exp2(own_top - top)
                    total = stat_ref[h, 1:2, columns] * factor + jnp.sum(p, 0, keepdims=True)
                    out = acc_ref[h, :, columns] * factor + dot(vt_ref[...], p.astype(BF16), NN)
                    o_ref[columns, h * HD : (h + 1) * HD] = (out / total).T.astype(BF16)


def partial_kernel(pos_ref, *refs, shares, kv, group):
    q_refs, (k_ref, v_ref, xk_ref, xv_ref, out_ref) = refs[:shares], refs[shares:]
    share = xk_ref.shape[0]
    width = group * share
    mine = pos_ref[0]
    row = lax.broadcasted_iota(jnp.int32, (share, width), 0)
    column = lax.broadcasted_iota(jnp.int32, (share, width), 1) % share
    for g in range(kv):
        lanes = slice(g * HD, (g + 1) * HD)
        keys, extra = k_ref[:, lanes], xk_ref[:, lanes]
        values, extra_values = v_ref[:, lanes].T, xv_ref[:, lanes].T
        for r in range(shares):
            source = lax.rem(mine - r + shares, shares)
            q = jnp.concatenate(
                [q_refs[r][:, (g * group + h) * HD : (g * group + h + 1) * HD] for h in range(group)], 0
            )
            s = dot(keys, q, NT)
            x = jnp.where(mine * share + row <= source * share + column, dot(extra, q, NT), MASKED)
            top = jnp.maximum(jnp.max(s, 0, keepdims=True), jnp.max(x, 0, keepdims=True)) * SCALE
            p, px = jnp.exp2(s * SCALE - top), jnp.exp2(x * SCALE - top)
            total = jnp.sum(p, 0, keepdims=True) + jnp.sum(px, 0, keepdims=True)
            acc = dot(values, p.astype(BF16), NN) + dot(extra_values, px.astype(BF16), NN)
            out_ref[r, g * width : (g + 1) * width, :] = acc.T
            out_ref[r, kv * width + 2 * g : kv * width + 2 * g + 1, :width] = top
            out_ref[r, kv * width + 2 * g + 1 : kv * width + 2 * g + 2, :width] = total


def merge_kernel(*refs, shares, kv, group):
    part_refs, out_ref = refs[:shares], refs[shares]
    share = out_ref.shape[0]
    width = group * share
    for g in range(kv):
        at = kv * width + 2 * g
        tops = [ref[0, at : at + 1, :width] for ref in part_refs]
        overall = functools.reduce(jnp.maximum, tops)
        factors = [jnp.exp2(top - overall) for top in tops]
        summed = sum(f * ref[0, at + 1 : at + 2, :width] for f, ref in zip(factors, part_refs))
        out = sum(
            f.reshape(width, 1) * ref[0, g * width : (g + 1) * width, :]
            for f, ref in zip(factors, part_refs)
        )
        out = (out / summed.reshape(width, 1)).astype(BF16)
        for h in range(group):
            out_ref[:, (g * group + h) * HD : (g * group + h + 1) * HD] = out[h * share : (h + 1) * share]


def body(context_queries, context_keys, context_values, query_queries, query_keys, query_values):
    rows = context_keys.shape[0]
    kv_device = context_keys.shape[1] // HD
    heads = context_queries.shape[1] // HD
    kv = max(kv_device // lax.axis_size("rep"), 1)
    group = heads // kv
    share = query_keys.shape[0]
    blocks = lax.axis_size("ctx")
    mine = lax.axis_index("ctx")
    offset = lax.axis_index("rep") * kv if kv_device > kv else jnp.int32(0)
    params = pltpu.CompilerParams(vmem_limit_bytes=VMEM_LIMIT)
    at_once = math.gcd(group, 4)

    parts = blocks - 1
    size = min(-(-rows // parts // 16) * 16, rows)
    starts = [min(r * size, rows - size) for r in range(parts)]

    def scatter(g):
        got = None
        for r in range(parts):
            piece = jnp.stack(
                [
                    lax.dynamic_slice(a, (starts[r], (offset + g) * HD), (size, HD))
                    for a in (context_keys, context_values)
                ]
            )
            sent = lax.ppermute(piece, "ctx", [(0, r + 1)])
            got = sent if got is None else jnp.where(mine == r + 1, sent, got)
        return got

    def exchange(part):
        return [part] + [
            lax.ppermute(part, "ctx", [(z + 1, (z + d) % parts + 1) for z in range(parts)])
            for d in range(1, parts)
        ]

    slot_part = [lax.rem(mine - 1 - d + 2 * parts, parts) for d in range(parts)]
    position = jnp.stack(
        [mine] + [jnp.minimum(part * size, rows - size) for part in slot_part]
    ).astype(jnp.int32)

    others = [
        lax.ppermute(query_queries, "ctx", [(z, (z + r) % blocks) for z in range(blocks)])
        for r in range(1, blocks)
    ]
    own_part = [scatter(g) for g in range(kv)]

    own_cost = pl.CostEstimate(
        flops=3 * heads * rows * rows * HD, bytes_accessed=8 * rows * heads * HD, transcendentals=0
    )
    per_kv = group // at_once
    acc, stats = pl.pallas_call(
        functools.partial(own_kernel, heads=at_once),
        grid_spec=pltpu.PrefetchScalarGridSpec(
            num_scalar_prefetch=1,
            grid=(heads // at_once,),
            in_specs=[
                pl.BlockSpec((rows, at_once * HD), lambda j, off: (0, j)),
                pl.BlockSpec((rows, HD), lambda j, off: (0, off[0] + j // per_kv)),
                pl.BlockSpec((rows, HD), lambda j, off: (0, off[0] + j // per_kv)),
            ],
            out_specs=[
                pl.BlockSpec((at_once, HD, rows), lambda j, off: (j, 0, 0)),
                pl.BlockSpec((at_once, 2, rows), lambda j, off: (j, 0, 0)),
            ],
        ),
        out_shape=[
            jax.ShapeDtypeStruct((heads, HD, rows), F32),
            jax.ShapeDtypeStruct((heads, 2, rows), F32),
        ],
        compiler_params=params,
        cost_estimate=own_cost,
        name="own",
    )(offset.reshape(1), context_queries, context_keys, context_values)

    pieces = [exchange(part) for part in own_part]

    payload_rows = -(-(kv * group * share + 2 * kv) // 8) * 8
    partial = pl.pallas_call(
        functools.partial(partial_kernel, shares=blocks, kv=kv, group=group),
        grid_spec=pltpu.PrefetchScalarGridSpec(
            num_scalar_prefetch=1,
            grid=(1,),
            in_specs=[pl.BlockSpec((share, heads * HD), lambda j, pos: (0, 0))] * blocks
            + [pl.BlockSpec((rows, kv * HD), lambda j, pos: (0, pos[1]))] * 2
            + [pl.BlockSpec((share, kv * HD), lambda j, pos: (0, pos[1]))] * 2,
            out_specs=pl.BlockSpec((blocks, payload_rows, HD), lambda j, pos: (0, 0, 0)),
        ),
        out_shape=jax.ShapeDtypeStruct((blocks, payload_rows, HD), F32),
        compiler_params=params,
        name="partial",
    )(
        jnp.stack([mine, offset // kv]).astype(jnp.int32),
        query_queries,
        *others,
        context_keys,
        context_values,
        query_keys,
        query_values,
    )
    returned = [partial[0:1]] + [
        lax.ppermute(partial[r : r + 1], "ctx", [(z, (z - r) % blocks) for z in range(blocks)])
        for r in range(1, blocks)
    ]

    context_out = None
    for g in range(kv):
        first = g * per_kv
        operands = [position, context_queries, acc, stats, *pieces[g]]
        in_specs = [
            pl.BlockSpec((rows, at_once * HD), lambda j, pos, first=first: (0, first + j)),
            pl.BlockSpec((at_once, HD, rows), lambda j, pos, first=first: (first + j, 0, 0)),
            pl.BlockSpec((at_once, 2, rows), lambda j, pos, first=first: (first + j, 0, 0)),
        ] + [pl.BlockSpec((2, size, HD), lambda j, pos: (0, 0, 0))] * parts
        if context_out is not None:
            operands.append(context_out)
            in_specs.append(pl.BlockSpec(memory_space=pl.ANY))
        context_out = pl.pallas_call(
            functools.partial(anchor_kernel, heads=at_once, parts=parts),
            grid_spec=pltpu.PrefetchScalarGridSpec(
                num_scalar_prefetch=1,
                grid=(per_kv,),
                in_specs=in_specs,
                out_specs=pl.BlockSpec(
                    (rows, at_once * HD), lambda j, pos, first=first: (0, first + j)
                ),
                scratch_shapes=[pltpu.VMEM((rows, HD), BF16), pltpu.VMEM((HD, rows), BF16)],
            ),
            out_shape=jax.ShapeDtypeStruct((rows, heads * HD), BF16),
            input_output_aliases={} if context_out is None else {len(operands) - 1: 0},
            compiler_params=params,
            cost_estimate=pl.CostEstimate(
                flops=4 * group * rows * rows * HD,
                bytes_accessed=8 * rows * group * HD,
                transcendentals=0,
            ),
            name="anchor",
        )(*operands)

    query_out = pl.pallas_call(
        functools.partial(merge_kernel, shares=blocks, kv=kv, group=group),
        out_shape=jax.ShapeDtypeStruct((share, heads * HD), BF16),
        compiler_params=params,
        name="merge",
    )(*returned)
    return context_out, query_out


def solution(mesh):
    in_specs = (
        P(("groups", "ctx"), ("kvh", "rep")),
        P(("groups", "ctx"), "kvh"),
        P(("groups", "ctx"), "kvh"),
        P(("groups", "ctx"), ("kvh", "rep")),
        P(("groups", "ctx"), "kvh"),
        P(("groups", "ctx"), "kvh"),
    )
    out_specs = (P(("groups", "ctx"), ("kvh", "rep")), P(("groups", "ctx"), ("kvh", "rep")))
    return jax.shard_map(body, mesh=mesh, in_specs=in_specs, out_specs=out_specs, check_vma=False)
```

```python
import functools
import math

import jax
import jax.numpy as jnp
from jax import lax
from jax.experimental import pallas as pl
from jax.experimental.pallas import tpu as pltpu
from jax.sharding import PartitionSpec as P

HD = 128
MASKED = -1e30
SCALE = math.log2(math.e) / math.sqrt(HD)
SAFE = 2.0**120
LIFT = 60.0
F32 = jnp.float32
BF16 = jnp.bfloat16
NT = (((1,), (1,)), ((), ()))
NN = (((1,), (0,)), ((), ()))
VMEM_LIMIT = 40 * 2**20


def dot(a, b, dims):
    return lax.dot_general(a, b, dims, preferred_element_type=F32)


def tile_of(length):
    return math.gcd(length, 256)


def in_turn(jobs, lead, score, soften, finish):
    jobs = list(jobs)
    leads = {t: lead(job) for t, job in enumerate(jobs[:2])}
    scores, weights = {0: score(jobs[0])}, {}
    for t in range(len(jobs) + 1):
        if t + 2 < len(jobs):
            leads[t + 2] = lead(jobs[t + 2])
        if t + 1 < len(jobs):
            scores[t + 1] = score(jobs[t + 1])
        if t < len(jobs):
            weights[t] = soften(jobs[t], leads.pop(t), scores.pop(t))
        if t > 0:
            finish(jobs[t - 1], weights.pop(t - 1))


def too_large(totals):
    return jnp.max(functools.reduce(jnp.maximum, [jnp.where(t < SAFE, 0.0, 1.0) for t in totals])) > 0.0


def own_kernel(off_ref, q_ref, k_ref, v_ref, *refs, heads):
    acc_ref, stat_ref = refs[-2:]
    rows = q_ref.shape[0]
    tile = tile_of(rows)
    sample = min(tile, 128)
    keys, values = k_ref[...], v_ref[...].T
    jobs = [(h, i) for h in range(heads) for i in range(rows // tile)]
    key = lax.broadcasted_iota(jnp.int32, (tile, tile), 0)
    causal = key <= lax.broadcasted_iota(jnp.int32, (tile, tile), 1)
    totals = []

    def query(job):
        h, i = job
        return q_ref[i * tile : (i + 1) * tile, h * HD : (h + 1) * HD]

    def lead(job):
        if job[1] == 0:
            return None
        return jnp.max(dot(keys[:sample], query(job), NT), 0, keepdims=True) * SCALE + LIFT

    def score(job):
        h, i = job
        before = [dot(keys[: i * tile], query(job), NT)] if i > 0 else []
        return before + [dot(keys[i * tile : (i + 1) * tile], query(job), NT)]

    def soften(job, top, scores):
        h, i = job
        if i == 0:
            s = jnp.where(causal, scores[0], MASKED)
            top = jnp.max(s, 0, keepdims=True) * SCALE + LIFT
            p = [jnp.exp2(s * SCALE - top)]
        else:
            p = [jnp.exp2(s * SCALE - top) for s in scores]
            p[1] = jnp.where(causal, p[1], 0.0)
        total = sum(jnp.sum(x, 0, keepdims=True) for x in p)
        p = [x.astype(BF16) for x in p]
        return jnp.concatenate(p, 0) if i > 0 else p[0], top, total

    def finish(job, state):
        h, i = job
        p, top, total = state
        columns = slice(i * tile, (i + 1) * tile)
        acc_ref[h, :, columns] = dot(values[:, : (i + 1) * tile], p, NN)
        stat_ref[h, 0:1, columns] = top
        stat_ref[h, 1:2, columns] = total
        totals.append(total)

    in_turn(jobs, lead, score, soften, finish)

    @pl.when(too_large(totals))
    def _():
        for h in range(heads):

            @pl.loop(0, rows // tile)
            def _(i):
                columns = pl.ds(pl.multiple_of(i * tile, tile), tile)
                s = dot(k_ref[...], q_ref[columns, h * HD : (h + 1) * HD], NT) * SCALE
                at = lax.broadcasted_iota(jnp.int32, s.shape, 1) + i * tile
                s = jnp.where(lax.broadcasted_iota(jnp.int32, s.shape, 0) <= at, s, MASKED)
                top = jnp.max(s, 0, keepdims=True)
                p = jnp.exp2(s - top)
                acc_ref[h, :, columns] = dot(v_ref[...].T, p.astype(BF16), NN)
                stat_ref[h, 0:1, columns] = top
                stat_ref[h, 1:2, columns] = jnp.sum(p, 0, keepdims=True)


def anchor_kernel(pos_ref, q_ref, acc_ref, stat_ref, *refs, heads, copies, merge):
    o_ref, *query_ref, k_ref, v_ref, vt_ref, sem = refs[-6:] if merge else refs[-5:]
    copy_refs = refs[:copies]
    first = pl.program_id(0) == 0
    rows = q_ref.shape[0]
    tile = tile_of(rows)
    jobs = [(h, i) for h in range(heads) for i in range(rows // tile)]

    def fetch(act):
        for c, ref in enumerate(copy_refs):

            @pl.when(first & (pos_ref[0] == c))
            def _():
                for j, held in enumerate((k_ref, v_ref)):
                    act(pltpu.make_async_copy(ref.at[j], held, sem.at[j]))

    fetch(lambda copy: copy.start())
    if merge:
        returned = refs[copies : copies + merge["blocks"]]

        @pl.when(first)
        def _():
            merge_parts(returned, query_ref[0], kv=merge["kv"], group=merge["group"])

    fetch(lambda copy: copy.wait())

    @pl.when(pos_ref[0] < 0)
    def _():
        for h, i in jobs:
            columns = slice(i * tile, (i + 1) * tile)
            out = acc_ref[h, :, columns] / stat_ref[h, 1:2, columns]
            o_ref[columns, h * HD : (h + 1) * HD] = out.T.astype(BF16)

    @pl.when(pos_ref[0] >= 0)
    def _():
        @pl.when(first)
        def _():
            vt_ref[...] = v_ref[...].T

        keys, values = k_ref[...], vt_ref[...]
        totals = []

        def score(job):
            h, i = job
            return dot(keys, q_ref[i * tile : (i + 1) * tile, h * HD : (h + 1) * HD], NT)

        def soften(job, _, s):
            h, i = job
            columns = slice(i * tile, (i + 1) * tile)
            p = jnp.exp2(s * SCALE - stat_ref[h, 0:1, columns])
            return p.astype(BF16), stat_ref[h, 1:2, columns] + jnp.sum(p, 0, keepdims=True)

        def finish(job, state):
            h, i = job
            p, total = state
            columns = slice(i * tile, (i + 1) * tile)
            out = acc_ref[h, :, columns] + dot(values, p, NN)
            o_ref[columns, h * HD : (h + 1) * HD] = (out / total).T.astype(BF16)
            totals.append(total)

        in_turn(jobs, lambda job: None, score, soften, finish)

        @pl.when(too_large(totals))
        def _():
            for h in range(heads):

                @pl.loop(0, rows // tile)
                def _(i):
                    columns = pl.ds(pl.multiple_of(i * tile, tile), tile)
                    s = dot(k_ref[...], q_ref[columns, h * HD : (h + 1) * HD], NT) * SCALE
                    own_top = stat_ref[h, 0:1, columns]
                    top = jnp.maximum(own_top, jnp.max(s, 0, keepdims=True))
                    p = jnp.exp2(s - top)
                    factor = jnp.exp2(own_top - top)
                    total = stat_ref[h, 1:2, columns] * factor + jnp.sum(p, 0, keepdims=True)
                    out = acc_ref[h, :, columns] * factor + dot(vt_ref[...], p.astype(BF16), NN)
                    o_ref[columns, h * HD : (h + 1) * HD] = (out / total).T.astype(BF16)


def partial_kernel(lanes_ref, mine_ref, *refs, shares, kv, group):
    out_refs = refs[-shares:]
    *q_refs, k_ref, v_ref, xk_ref, xv_ref = refs[:-shares]
    share = xk_ref.shape[0]
    slots = [(ref, i) for ref in q_refs for i in range(0, ref.shape[0], share)]
    width = group * share
    mine = mine_ref[0]
    together = max(1, min(shares, 256 // width))
    row = lax.broadcasted_iota(jnp.int32, (share, together * width), 0)
    column = lax.broadcasted_iota(jnp.int32, (share, together * width), 1)

    def visible(r):
        source = (r + column // width) ^ mine
        return mine * share + row <= source * share + column % share

    packs = [(g, r) for g in range(kv) for r in range(0, shares, together)]

    def lanes(g):
        return slice(g * HD, (g + 1) * HD)

    def score(job):
        g, r = job
        q = jnp.concatenate(
            [
                ref[i : i + share, (g * group + h) * HD : (g * group + h + 1) * HD]
                for ref, i in slots[r : r + together]
                for h in range(group)
            ],
            0,
        )
        return dot(k_ref[:, lanes(g)], q, NT), dot(xk_ref[:, lanes(g)], q, NT)

    def soften(job, _, scores):
        g, r = job
        s, x = scores
        x = jnp.where(visible(r), x, MASKED)
        top = jnp.maximum(jnp.max(s, 0, keepdims=True), jnp.max(x, 0, keepdims=True)) * SCALE
        p, px = jnp.exp2(s * SCALE - top), jnp.exp2(x * SCALE - top)
        total = jnp.sum(p, 0, keepdims=True) + jnp.sum(px, 0, keepdims=True)
        return p.astype(BF16), px.astype(BF16), top, total

    def finish(job, state):
        g, r = job
        p, px, top, total = state
        acc = dot(v_ref[:, lanes(g)].T, p, NN) + dot(xv_ref[:, lanes(g)].T, px, NN)
        at = kv * width + 2 * g
        for c in range(together):
            columns = slice(c * width, (c + 1) * width)
            out_ref = out_refs[r + c]
            out_ref[g * width : (g + 1) * width, :] = acc[:, columns].T
            out_ref[at : at + 1, :width] = top[:, columns]
            out_ref[at + 1 : at + 2, :width] = total[:, columns]

    in_turn(packs, lambda job: None, score, soften, finish)


def merge_parts(part_refs, out_ref, *, kv, group):
    share = out_ref.shape[0]
    width = group * share
    for g in range(kv):
        at = kv * width + 2 * g
        tops = [ref[at : at + 1, :width] for ref in part_refs]
        overall = functools.reduce(jnp.maximum, tops)
        factors = [jnp.exp2(top - overall) for top in tops]
        summed = sum(f * ref[at + 1 : at + 2, :width] for f, ref in zip(factors, part_refs))
        out = sum(
            (f / summed).reshape(width, 1) * ref[g * width : (g + 1) * width, :]
            for f, ref in zip(factors, part_refs)
        ).astype(BF16)
        for h in range(group):
            out_ref[:, (g * group + h) * HD : (g * group + h + 1) * HD] = out[h * share : (h + 1) * share]


def relay(blocks):
    half = blocks // 2
    hops, holders = [[[(0, half)]]], [half]
    while half > 1:
        half //= 2
        hops.append([[(z, z - half) for z in holders], [(z, z + half) for z in holders]])
        holders = holders + [z + sign * half for z in holders for sign in (-1, 1)]
        holders = [z for z in holders if z % half == 0 and (z // half) % 2 == 1]
    return hops


def in_hbm(*arrays):
    return [pltpu.with_memory_space_constraint(a, pltpu.HBM) for a in arrays]


def body(context_queries, context_keys, context_values, query_queries, query_keys, query_values):
    rows = context_keys.shape[0]
    kv_device = context_keys.shape[1] // HD
    heads = context_queries.shape[1] // HD
    kv = max(kv_device // lax.axis_size("rep"), 1)
    group = heads // kv
    share = query_keys.shape[0]
    blocks = lax.axis_size("ctx")
    mine = lax.axis_index("ctx")
    offset = lax.axis_index("rep") * kv if kv_device > kv else jnp.int32(0)
    params = pltpu.CompilerParams(vmem_limit_bytes=VMEM_LIMIT)
    at_once = math.gcd(group, 2)
    steps = group // at_once

    own_copy = [
        jnp.stack(
            [
                lax.dynamic_slice(a, (0, (offset + g) * HD), (rows, HD))
                for a in (context_keys, context_values)
            ]
        )
        for g in range(kv)
    ]
    hops = relay(blocks)
    taken = [-1] * blocks
    for c, pairs in enumerate(p for some in hops for p in some):
        for _, z in pairs:
            taken[z] = c
    taken = sum(jnp.where(mine == z, c, 0) for z, c in enumerate(taken))
    received = [[] for _ in range(kv)]

    def step(s):
        transfers = []
        pieces = [own_copy[g] if s == g or not received[g] else held(g) for g in range(kv)]
        for g in range(kv):
            for pairs in hops[s - g] if 0 <= s - g < len(hops) else ():
                for transfer in transfers:
                    ends = [pair for _, other in transfer for pair in other]
                    if all(p[0] != e[0] and p[1] != e[1] for p in pairs for e in ends):
                        transfer.append((g, pairs))
                        break
                else:
                    transfers.append([(g, pairs)])
        for transfer in transfers:
            operand = None
            for g, pairs in transfer:
                piece = pieces[g]
                sends = functools.reduce(jnp.logical_or, [mine == p[0] for p in pairs])
                operand = piece if operand is None else jnp.where(sends, piece, operand)
            got = lax.ppermute(operand, "ctx", [p for _, pairs in transfer for p in pairs])
            for g, pairs in transfer:
                received[g].append(got)

    def held(g):
        piece = received[g][0]
        for c in range(1, len(received[g])):
            piece = jnp.where(taken == c, received[g][c], piece)
        return piece

    def own(begin, end, queries, sums):
        return pl.pallas_call(
            functools.partial(own_kernel, heads=at_once),
            grid_spec=pltpu.PrefetchScalarGridSpec(
                num_scalar_prefetch=1,
                grid=(end - begin,),
                in_specs=[pl.BlockSpec((rows, at_once * HD), lambda j, off: (0, begin + j))]
                + [pl.BlockSpec((rows, HD), lambda j, off: (0, off[0] + (begin + j) // steps))] * 2
                + [pl.BlockSpec(memory_space=pl.ANY)] * len(sums),
                out_specs=[
                    pl.BlockSpec((at_once, HD, rows), lambda j, off: (begin + j, 0, 0)),
                    pl.BlockSpec((at_once, 2, rows), lambda j, off: (begin + j, 0, 0)),
                ],
            ),
            out_shape=[
                pltpu.HBM((heads, HD, rows), F32),
                pltpu.HBM((heads, 2, rows), F32),
            ],
            input_output_aliases={4 + i: i for i in range(len(sums))},
            compiler_params=params,
            cost_estimate=pl.CostEstimate(
                flops=4 * (end - begin) * at_once * rows * rows * HD,
                bytes_accessed=8 * rows * (end - begin) * at_once * HD,
                transcendentals=0,
            ),
            name="own",
        )(offset.reshape(1), *in_hbm(queries, context_keys, context_values, *sums))

    queries = context_queries
    slots = [query_queries] + [
        lax.ppermute(query_queries, "ctx", [(z, z ^ r) for z in range(blocks)]) for r in range(1, blocks)
    ]
    step(0)
    total = heads // at_once
    early = -(-3 * total // 4)
    sums, slots, received, queries = lax.optimization_barrier(
        (own(0, early, queries, ()), slots, received, queries)
    )
    step(1)
    payload_rows = -(-(kv * group * share + 2 * kv) // 8) * 8
    partial = pl.pallas_call(
        functools.partial(partial_kernel, shares=blocks, kv=kv, group=group),
        grid_spec=pltpu.PrefetchScalarGridSpec(
            num_scalar_prefetch=2,
            grid=(1,),
            in_specs=[pl.BlockSpec(q.shape, lambda j, at, pos: (0, 0)) for q in slots]
            + [pl.BlockSpec((rows, kv * HD), lambda j, at, pos: (0, at[0]))] * 2
            + [pl.BlockSpec((share, kv * HD), lambda j, at, pos: (0, at[0]))] * 2,
            out_specs=[pl.BlockSpec((payload_rows, HD), lambda j, at, pos: (0, 0))] * blocks,
        ),
        out_shape=[jax.ShapeDtypeStruct((payload_rows, HD), F32)] * blocks,
        compiler_params=params,
        name="partial",
    )(
        (offset // kv).reshape(1),
        mine.reshape(1),
        *slots,
        *in_hbm(context_keys, context_values),
        query_keys,
        query_values,
    )
    partial, sums, queries = lax.optimization_barrier((partial, sums, queries))
    returned = [
        lax.ppermute(partial[r], "ctx", [(z, z ^ r) for z in range(blocks)]) for r in range(1, blocks)
    ]
    if early < total:
        sums = own(early, total, queries, sums)
    for s in range(2, kv + len(hops) - 1):
        sums, received = lax.optimization_barrier((sums, received))
        step(s)
    sums, returned = lax.optimization_barrier((sums, returned))
    returned = [partial[0]] + returned

    context_out = query_out = None
    for g in range(kv):
        last = g == kv - 1
        operands = [taken.reshape(1), *in_hbm(context_queries, *sums), *received[g]]
        in_specs = [
            pl.BlockSpec((rows, at_once * HD), lambda j, pos, g=g: (0, g * steps + j)),
            pl.BlockSpec((at_once, HD, rows), lambda j, pos, g=g: (g * steps + j, 0, 0)),
            pl.BlockSpec((at_once, 2, rows), lambda j, pos, g=g: (g * steps + j, 0, 0)),
        ] + [pl.BlockSpec(memory_space=pl.ANY)] * len(received[g])
        out_specs = [pl.BlockSpec((rows, at_once * HD), lambda j, pos, g=g: (0, g * steps + j))]
        out_shape = [jax.ShapeDtypeStruct((rows, heads * HD), BF16)]
        if last:
            operands += returned
            in_specs += [pl.BlockSpec((payload_rows, HD), lambda j, pos: (0, 0))] * blocks
            out_specs.append(pl.BlockSpec((share, heads * HD), lambda j, pos: (0, 0)))
            out_shape.append(jax.ShapeDtypeStruct((share, heads * HD), BF16))
        if g > 0:
            operands += in_hbm(context_out)
            in_specs.append(pl.BlockSpec(memory_space=pl.ANY))
        out = pl.pallas_call(
            functools.partial(
                anchor_kernel,
                heads=at_once,
                copies=len(received[g]),
                merge=dict(blocks=blocks, kv=kv, group=group) if last else None,
            ),
            grid_spec=pltpu.PrefetchScalarGridSpec(
                num_scalar_prefetch=1,
                grid=(steps,),
                in_specs=in_specs,
                out_specs=out_specs,
                scratch_shapes=[
                    pltpu.VMEM((rows, HD), BF16),
                    pltpu.VMEM((rows, HD), BF16),
                    pltpu.VMEM((HD, rows), BF16),
                    pltpu.SemaphoreType.DMA((2,)),
                ],
            ),
            out_shape=out_shape,
            input_output_aliases={len(operands) - 1: 0} if g > 0 else {},
            compiler_params=params,
            cost_estimate=pl.CostEstimate(
                flops=4 * group * rows * rows * HD, bytes_accessed=8 * rows * group * HD, transcendentals=0
            ),
            name="anchor",
        )(*operands)
        context_out = out[0]
        query_out = out[-1]
    return context_out, query_out


def solution(mesh):
    in_specs = (
        P(("groups", "ctx"), ("kvh", "rep")),
        P(("groups", "ctx"), "kvh"),
        P(("groups", "ctx"), "kvh"),
        P(("groups", "ctx"), ("kvh", "rep")),
        P(("groups", "ctx"), "kvh"),
        P(("groups", "ctx"), "kvh"),
    )
    out_specs = (P(("groups", "ctx"), ("kvh", "rep")), P(("groups", "ctx"), ("kvh", "rep")))
    return jax.shard_map(body, mesh=mesh, in_specs=in_specs, out_specs=out_specs, check_vma=False)
```

```python
import functools
import math

import jax
import jax.numpy as jnp
from jax import lax
from jax.experimental import pallas as pl
from jax.experimental.pallas import tpu as pltpu
from jax.sharding import PartitionSpec as P

HD = 128
MASKED = -1e30
SCALE = math.log2(math.e) / math.sqrt(HD)
SAFE = 2.0**120
LIFT = 60.0
F32 = jnp.float32
BF16 = jnp.bfloat16
NT = (((1,), (1,)), ((), ()))
NN = (((1,), (0,)), ((), ()))
VMEM_LIMIT = 40 * 2**20


def dot(a, b, dims):
    return lax.dot_general(a, b, dims, preferred_element_type=F32)


def tile_of(length):
    return math.gcd(length, 256)


def in_turn(jobs, lead, score, soften, finish):
    jobs = list(jobs)
    leads = {t: lead(job) for t, job in enumerate(jobs[:2])}
    scores, weights = {0: score(jobs[0])}, {}
    for t in range(len(jobs) + 1):
        if t + 2 < len(jobs):
            leads[t + 2] = lead(jobs[t + 2])
        if t + 1 < len(jobs):
            scores[t + 1] = score(jobs[t + 1])
        if t < len(jobs):
            weights[t] = soften(jobs[t], leads.pop(t), scores.pop(t))
        if t > 0:
            finish(jobs[t - 1], weights.pop(t - 1))


def too_large(totals):
    return jnp.max(functools.reduce(jnp.maximum, [jnp.where(t < SAFE, 0.0, 1.0) for t in totals])) > 0.0


def own_kernel(off_ref, q_ref, k_ref, v_ref, *refs, heads):
    acc_ref, stat_ref = refs[-2:]
    rows = q_ref.shape[0]
    tile = tile_of(rows)
    sample = min(tile, 128)
    keys, values = k_ref[...], v_ref[...].T
    jobs = [(h, i) for h in range(heads) for i in range(rows // tile)]
    key = lax.broadcasted_iota(jnp.int32, (tile, tile), 0)
    causal = key <= lax.broadcasted_iota(jnp.int32, (tile, tile), 1)
    totals = []

    def query(job):
        h, i = job
        return q_ref[i * tile : (i + 1) * tile, h * HD : (h + 1) * HD]

    def lead(job):
        if job[1] == 0:
            return None
        return jnp.max(dot(keys[:sample], query(job), NT), 0, keepdims=True) * SCALE + LIFT

    def score(job):
        h, i = job
        before = [dot(keys[: i * tile], query(job), NT)] if i > 0 else []
        return before + [dot(keys[i * tile : (i + 1) * tile], query(job), NT)]

    def soften(job, top, scores):
        h, i = job
        if i == 0:
            s = jnp.where(causal, scores[0], MASKED)
            top = jnp.max(s, 0, keepdims=True) * SCALE + LIFT
            p = [jnp.exp2(s * SCALE - top)]
        else:
            p = [jnp.exp2(s * SCALE - top) for s in scores]
            p[1] = jnp.where(causal, p[1], 0.0)
        total = sum(jnp.sum(x, 0, keepdims=True) for x in p)
        p = [x.astype(BF16) for x in p]
        return jnp.concatenate(p, 0) if i > 0 else p[0], top, total

    def finish(job, state):
        h, i = job
        p, top, total = state
        columns = slice(i * tile, (i + 1) * tile)
        acc_ref[h, :, columns] = dot(values[:, : (i + 1) * tile], p, NN)
        stat_ref[h, 0:1, columns] = top
        stat_ref[h, 1:2, columns] = total
        totals.append(total)

    in_turn(jobs, lead, score, soften, finish)

    @pl.when(too_large(totals))
    def _():
        for h in range(heads):

            @pl.loop(0, rows // tile)
            def _(i):
                columns = pl.ds(pl.multiple_of(i * tile, tile), tile)
                s = dot(k_ref[...], q_ref[columns, h * HD : (h + 1) * HD], NT) * SCALE
                at = lax.broadcasted_iota(jnp.int32, s.shape, 1) + i * tile
                s = jnp.where(lax.broadcasted_iota(jnp.int32, s.shape, 0) <= at, s, MASKED)
                top = jnp.max(s, 0, keepdims=True)
                p = jnp.exp2(s - top)
                acc_ref[h, :, columns] = dot(v_ref[...].T, p.astype(BF16), NN)
                stat_ref[h, 0:1, columns] = top
                stat_ref[h, 1:2, columns] = jnp.sum(p, 0, keepdims=True)


def anchor_kernel(pos_ref, q_ref, acc_ref, stat_ref, *refs, heads, copies, merge):
    o_ref, *query_ref, k_ref, v_ref, vt_ref, sem = refs[-6:] if merge else refs[-5:]
    copy_refs = refs[:copies]
    first = pl.program_id(0) == 0
    rows = q_ref.shape[0]
    tile = tile_of(rows)
    jobs = [(h, i) for h in range(heads) for i in range(rows // tile)]

    def fetch(act):
        for c, ref in enumerate(copy_refs):

            @pl.when(first & (pos_ref[0] == c))
            def _():
                for j, held in enumerate((k_ref, v_ref)):
                    act(pltpu.make_async_copy(ref.at[j], held, sem.at[j]))

    fetch(lambda copy: copy.start())
    if merge:
        returned = refs[copies : copies + merge["blocks"]]

        @pl.when(first)
        def _():
            merge_parts(returned, query_ref[0], kv=merge["kv"], group=merge["group"])

    fetch(lambda copy: copy.wait())

    @pl.when(pos_ref[0] < 0)
    def _():
        for h, i in jobs:
            columns = slice(i * tile, (i + 1) * tile)
            out = acc_ref[h, :, columns] / stat_ref[h, 1:2, columns]
            o_ref[columns, h * HD : (h + 1) * HD] = out.T.astype(BF16)

    @pl.when(pos_ref[0] >= 0)
    def _():
        @pl.when(first)
        def _():
            vt_ref[...] = v_ref[...].T

        keys, values = k_ref[...], vt_ref[...]
        totals = []

        def score(job):
            h, i = job
            return dot(keys, q_ref[i * tile : (i + 1) * tile, h * HD : (h + 1) * HD], NT)

        def soften(job, _, s):
            h, i = job
            columns = slice(i * tile, (i + 1) * tile)
            p = jnp.exp2(s * SCALE - stat_ref[h, 0:1, columns])
            return p.astype(BF16), stat_ref[h, 1:2, columns] + jnp.sum(p, 0, keepdims=True)

        def finish(job, state):
            h, i = job
            p, total = state
            columns = slice(i * tile, (i + 1) * tile)
            out = acc_ref[h, :, columns] + dot(values, p, NN)
            o_ref[columns, h * HD : (h + 1) * HD] = (out / total).T.astype(BF16)
            totals.append(total)

        in_turn(jobs, lambda job: None, score, soften, finish)

        @pl.when(too_large(totals))
        def _():
            for h in range(heads):

                @pl.loop(0, rows // tile)
                def _(i):
                    columns = pl.ds(pl.multiple_of(i * tile, tile), tile)
                    s = dot(k_ref[...], q_ref[columns, h * HD : (h + 1) * HD], NT) * SCALE
                    own_top = stat_ref[h, 0:1, columns]
                    top = jnp.maximum(own_top, jnp.max(s, 0, keepdims=True))
                    p = jnp.exp2(s - top)
                    factor = jnp.exp2(own_top - top)
                    total = stat_ref[h, 1:2, columns] * factor + jnp.sum(p, 0, keepdims=True)
                    out = acc_ref[h, :, columns] * factor + dot(vt_ref[...], p.astype(BF16), NN)
                    o_ref[columns, h * HD : (h + 1) * HD] = (out / total).T.astype(BF16)


def partial_kernel(lanes_ref, mine_ref, *refs, shares, kv, group):
    out_refs = refs[-shares:]
    *q_refs, k_ref, v_ref, xk_ref, xv_ref = refs[:-shares]
    share = xk_ref.shape[0]
    slots = [(ref, i) for ref in q_refs for i in range(0, ref.shape[0], share)]
    width = group * share
    mine = mine_ref[0]
    together = max(1, min(shares, 256 // width))
    row = lax.broadcasted_iota(jnp.int32, (share, together * width), 0)
    column = lax.broadcasted_iota(jnp.int32, (share, together * width), 1)

    def visible(r):
        source = (r + column // width) ^ mine
        return mine * share + row <= source * share + column % share

    packs = [(g, r) for g in range(kv) for r in range(0, shares, together)]

    def lanes(g):
        return slice(g * HD, (g + 1) * HD)

    def score(job):
        g, r = job
        q = jnp.concatenate(
            [
                ref[i : i + share, (g * group + h) * HD : (g * group + h + 1) * HD]
                for ref, i in slots[r : r + together]
                for h in range(group)
            ],
            0,
        )
        return dot(k_ref[:, lanes(g)], q, NT), dot(xk_ref[:, lanes(g)], q, NT)

    def soften(job, _, scores):
        g, r = job
        s, x = scores
        x = jnp.where(visible(r), x, MASKED)
        top = jnp.maximum(jnp.max(s, 0, keepdims=True), jnp.max(x, 0, keepdims=True)) * SCALE
        p, px = jnp.exp2(s * SCALE - top), jnp.exp2(x * SCALE - top)
        total = jnp.sum(p, 0, keepdims=True) + jnp.sum(px, 0, keepdims=True)
        return p.astype(BF16), px.astype(BF16), top, total

    def finish(job, state):
        g, r = job
        p, px, top, total = state
        acc = dot(v_ref[:, lanes(g)].T, p, NN) + dot(xv_ref[:, lanes(g)].T, px, NN)
        at = kv * width + 2 * g
        for c in range(together):
            columns = slice(c * width, (c + 1) * width)
            out_ref = out_refs[r + c]
            out_ref[g * width : (g + 1) * width, :] = acc[:, columns].T
            out_ref[at : at + 1, :width] = top[:, columns]
            out_ref[at + 1 : at + 2, :width] = total[:, columns]

    in_turn(packs, lambda job: None, score, soften, finish)


def merge_parts(part_refs, out_ref, *, kv, group):
    share = out_ref.shape[0]
    width = group * share
    for g in range(kv):
        at = kv * width + 2 * g
        tops = [ref[at : at + 1, :width] for ref in part_refs]
        overall = functools.reduce(jnp.maximum, tops)
        factors = [jnp.exp2(top - overall) for top in tops]
        summed = sum(f * ref[at + 1 : at + 2, :width] for f, ref in zip(factors, part_refs))
        out = sum(
            (f / summed).reshape(width, 1) * ref[g * width : (g + 1) * width, :]
            for f, ref in zip(factors, part_refs)
        ).astype(BF16)
        for h in range(group):
            out_ref[:, (g * group + h) * HD : (g * group + h + 1) * HD] = out[h * share : (h + 1) * share]


def relay(blocks, last):
    half = blocks // 2
    hops, holders = [[[(0, half)]]], [half]
    while half > 1:
        half //= 2
        if last and half == 1:
            hops.append([[(z, z + 1) for z in range(0, blocks, 2)]])
            break
        hops.append([[(z, z - half) for z in holders], [(z, z + half) for z in holders]])
        holders = [z + sign * half for z in holders for sign in (-1, 1)]
    return hops


def in_hbm(*arrays):
    return [pltpu.with_memory_space_constraint(a, pltpu.HBM) for a in arrays]


def body(context_queries, context_keys, context_values, query_queries, query_keys, query_values):
    rows = context_keys.shape[0]
    kv_device = context_keys.shape[1] // HD
    heads = context_queries.shape[1] // HD
    kv = max(kv_device // lax.axis_size("rep"), 1)
    group = heads // kv
    share = query_keys.shape[0]
    blocks = lax.axis_size("ctx")
    mine = lax.axis_index("ctx")
    offset = lax.axis_index("rep") * kv if kv_device > kv else jnp.int32(0)
    params = pltpu.CompilerParams(vmem_limit_bytes=VMEM_LIMIT)
    at_once = math.gcd(group, 2)
    steps = group // at_once

    own_copy = [
        jnp.stack(
            [
                lax.dynamic_slice(a, (0, (offset + g) * HD), (rows, HD))
                for a in (context_keys, context_values)
            ]
        )
        for g in range(kv)
    ]
    hops = [relay(blocks, g == kv - 1) for g in range(kv)]
    levels = len(hops[0])
    received = [[] for _ in range(kv)]

    def chosen(g):
        copies = [pairs for some in hops[g] for pairs in some]
        return sum(
            jnp.where(mine == z, c + 1, 0) for c, pairs in enumerate(copies) for _, z in pairs
        ) - 1

    taken = [chosen(g) for g in range(kv)]

    def step(s):
        transfers = []
        for g in range(kv):
            for pairs in hops[g][s - g] if 0 <= s - g < levels else ():
                for transfer in transfers:
                    ends = [pair for _, other in transfer for pair in other]
                    if all(p[0] != e[0] and p[1] != e[1] for p in pairs for e in ends):
                        transfer.append((g, pairs))
                        break
                else:
                    transfers.append([(g, pairs)])
        pieces = {(g, pairs[0]): held(g, pairs) for transfer in transfers for g, pairs in transfer}
        for transfer in transfers:
            operand = None
            for g, pairs in transfer:
                piece = pieces[g, pairs[0]]
                sends = functools.reduce(jnp.logical_or, [mine == p[0] for p in pairs])
                operand = piece if operand is None else jnp.where(sends, piece, operand)
            got = lax.ppermute(operand, "ctx", [p for _, pairs in transfer for p in pairs])
            for g, pairs in transfer:
                received[g].append(got)

    def held(g, pairs):
        if not received[g]:
            return own_copy[g]
        piece = received[g][0]
        for c in range(1, len(received[g])):
            piece = jnp.where(taken[g] == c, received[g][c], piece)
        return jnp.where(mine == 0, own_copy[g], piece) if pairs[0][0] == 0 else piece

    def own(begin, end, queries, sums):
        return pl.pallas_call(
            functools.partial(own_kernel, heads=at_once),
            grid_spec=pltpu.PrefetchScalarGridSpec(
                num_scalar_prefetch=1,
                grid=(end - begin,),
                in_specs=[pl.BlockSpec((rows, at_once * HD), lambda j, off: (0, begin + j))]
                + [pl.BlockSpec((rows, HD), lambda j, off: (0, off[0] + (begin + j) // steps))] * 2
                + [pl.BlockSpec(memory_space=pl.ANY)] * len(sums),
                out_specs=[
                    pl.BlockSpec((at_once, HD, rows), lambda j, off: (begin + j, 0, 0)),
                    pl.BlockSpec((at_once, 2, rows), lambda j, off: (begin + j, 0, 0)),
                ],
            ),
            out_shape=[
                pltpu.HBM((heads, HD, rows), F32),
                pltpu.HBM((heads, 2, rows), F32),
            ],
            input_output_aliases={4 + i: i for i in range(len(sums))},
            compiler_params=params,
            cost_estimate=pl.CostEstimate(
                flops=4 * (end - begin) * at_once * rows * rows * HD,
                bytes_accessed=8 * rows * (end - begin) * at_once * HD,
                transcendentals=0,
            ),
            name="own",
        )(offset.reshape(1), *in_hbm(queries, context_keys, context_values, *sums))

    queries = context_queries
    slots = [query_queries] + [
        lax.ppermute(query_queries, "ctx", [(z, z ^ r) for z in range(blocks)]) for r in range(1, blocks)
    ]
    step(0)
    total = heads // at_once
    early = -(-3 * total // 4)
    sums, slots, received, queries = lax.optimization_barrier(
        (own(0, early, queries, ()), slots, received, queries)
    )
    step(1)
    payload_rows = -(-(kv * group * share + 2 * kv) // 8) * 8
    partial = pl.pallas_call(
        functools.partial(partial_kernel, shares=blocks, kv=kv, group=group),
        grid_spec=pltpu.PrefetchScalarGridSpec(
            num_scalar_prefetch=2,
            grid=(1,),
            in_specs=[pl.BlockSpec(q.shape, lambda j, at, pos: (0, 0)) for q in slots]
            + [pl.BlockSpec((rows, kv * HD), lambda j, at, pos: (0, at[0]))] * 2
            + [pl.BlockSpec((share, kv * HD), lambda j, at, pos: (0, at[0]))] * 2,
            out_specs=[pl.BlockSpec((payload_rows, HD), lambda j, at, pos: (0, 0))] * blocks,
        ),
        out_shape=[jax.ShapeDtypeStruct((payload_rows, HD), F32)] * blocks,
        compiler_params=params,
        name="partial",
    )(
        (offset // kv).reshape(1),
        mine.reshape(1),
        *slots,
        *in_hbm(context_keys, context_values),
        query_keys,
        query_values,
    )
    partial, sums, queries = lax.optimization_barrier((partial, sums, queries))
    if early < total:
        sums = own(early, total, queries, sums)
    for s in range(2, kv + levels - 1):
        sums, received, partial = lax.optimization_barrier((sums, received, partial))
        step(s)
    returned = [
        lax.ppermute(partial[r], "ctx", [(z, z ^ r) for z in range(blocks)]) for r in range(1, blocks)
    ]
    returned = [partial[0]] + returned

    context_out = query_out = None
    for g in range(kv):
        last = g == kv - 1
        operands = [taken[g].reshape(1), *in_hbm(context_queries, *sums), *received[g]]
        in_specs = [
            pl.BlockSpec((rows, at_once * HD), lambda j, pos, g=g: (0, g * steps + j)),
            pl.BlockSpec((at_once, HD, rows), lambda j, pos, g=g: (g * steps + j, 0, 0)),
            pl.BlockSpec((at_once, 2, rows), lambda j, pos, g=g: (g * steps + j, 0, 0)),
        ] + [pl.BlockSpec(memory_space=pl.ANY)] * len(received[g])
        out_specs = [pl.BlockSpec((rows, at_once * HD), lambda j, pos, g=g: (0, g * steps + j))]
        out_shape = [jax.ShapeDtypeStruct((rows, heads * HD), BF16)]
        if last:
            operands += returned
            in_specs += [pl.BlockSpec((payload_rows, HD), lambda j, pos: (0, 0))] * blocks
            out_specs.append(pl.BlockSpec((share, heads * HD), lambda j, pos: (0, 0)))
            out_shape.append(jax.ShapeDtypeStruct((share, heads * HD), BF16))
        if g > 0:
            operands += in_hbm(context_out)
            in_specs.append(pl.BlockSpec(memory_space=pl.ANY))
        out = pl.pallas_call(
            functools.partial(
                anchor_kernel,
                heads=at_once,
                copies=len(received[g]),
                merge=dict(blocks=blocks, kv=kv, group=group) if last else None,
            ),
            grid_spec=pltpu.PrefetchScalarGridSpec(
                num_scalar_prefetch=1,
                grid=(steps,),
                in_specs=in_specs,
                out_specs=out_specs,
                scratch_shapes=[
                    pltpu.VMEM((rows, HD), BF16),
                    pltpu.VMEM((rows, HD), BF16),
                    pltpu.VMEM((HD, rows), BF16),
                    pltpu.SemaphoreType.DMA((2,)),
                ],
            ),
            out_shape=out_shape,
            input_output_aliases={len(operands) - 1: 0} if g > 0 else {},
            compiler_params=params,
            cost_estimate=pl.CostEstimate(
                flops=4 * group * rows * rows * HD, bytes_accessed=8 * rows * group * HD, transcendentals=0
            ),
            name="anchor",
        )(*operands)
        context_out = out[0]
        query_out = out[-1]
    return context_out, query_out


def solution(mesh):
    in_specs = (
        P(("groups", "ctx"), ("kvh", "rep")),
        P(("groups", "ctx"), "kvh"),
        P(("groups", "ctx"), "kvh"),
        P(("groups", "ctx"), ("kvh", "rep")),
        P(("groups", "ctx"), "kvh"),
        P(("groups", "ctx"), "kvh"),
    )
    out_specs = (P(("groups", "ctx"), ("kvh", "rep")), P(("groups", "ctx"), ("kvh", "rep")))
    return jax.shard_map(body, mesh=mesh, in_specs=in_specs, out_specs=out_specs, check_vma=False)
```

```python
import functools
import math

import jax
import jax.numpy as jnp
from jax import lax
from jax.experimental import pallas as pl
from jax.experimental.pallas import tpu as pltpu
from jax.sharding import PartitionSpec as P

HD = 128
MASKED = -1e30
SCALE = math.log2(math.e) / math.sqrt(HD)
SAFE = 2.0**120
LIFT = 60.0
F32 = jnp.float32
BF16 = jnp.bfloat16
NT = (((1,), (1,)), ((), ()))
NN = (((1,), (0,)), ((), ()))
VMEM_LIMIT = 40 * 2**20


def dot(a, b, dims):
    return lax.dot_general(a, b, dims, preferred_element_type=F32)


def tile_of(length):
    return math.gcd(length, 256)


def in_turn(jobs, lead, score, soften, finish):
    jobs = list(jobs)
    leads = {t: lead(job) for t, job in enumerate(jobs[:2])}
    scores, weights = {0: score(jobs[0])}, {}
    for t in range(len(jobs) + 1):
        if t + 2 < len(jobs):
            leads[t + 2] = lead(jobs[t + 2])
        if t + 1 < len(jobs):
            scores[t + 1] = score(jobs[t + 1])
        if t < len(jobs):
            weights[t] = soften(jobs[t], leads.pop(t), scores.pop(t))
        if t > 0:
            finish(jobs[t - 1], weights.pop(t - 1))


def too_large(totals):
    return jnp.max(functools.reduce(jnp.maximum, [jnp.where(t < SAFE, 0.0, 1.0) for t in totals])) > 0.0


def own_kernel(off_ref, q_ref, k_ref, v_ref, *refs, heads):
    acc_ref, stat_ref = refs[-2:]
    rows = q_ref.shape[0]
    tile = tile_of(rows)
    sample = min(tile, 128)
    keys, values = k_ref[...], v_ref[...].T
    jobs = [(h, i) for h in range(heads) for i in range(rows // tile)]
    key = lax.broadcasted_iota(jnp.int32, (tile, tile), 0)
    causal = key <= lax.broadcasted_iota(jnp.int32, (tile, tile), 1)
    totals = []

    def query(job):
        h, i = job
        return q_ref[i * tile : (i + 1) * tile, h * HD : (h + 1) * HD]

    def lead(job):
        if job[1] == 0:
            return None
        return jnp.max(dot(keys[:sample], query(job), NT), 0, keepdims=True) * SCALE + LIFT

    def score(job):
        h, i = job
        before = [dot(keys[: i * tile], query(job), NT)] if i > 0 else []
        return before + [dot(keys[i * tile : (i + 1) * tile], query(job), NT)]

    def soften(job, top, scores):
        h, i = job
        if i == 0:
            s = jnp.where(causal, scores[0], MASKED)
            top = jnp.max(s, 0, keepdims=True) * SCALE + LIFT
            p = [jnp.exp2(s * SCALE - top)]
        else:
            p = [jnp.exp2(s * SCALE - top) for s in scores]
            p[1] = jnp.where(causal, p[1], 0.0)
        total = sum(jnp.sum(x, 0, keepdims=True) for x in p)
        p = [x.astype(BF16) for x in p]
        return jnp.concatenate(p, 0) if i > 0 else p[0], top, total

    def finish(job, state):
        h, i = job
        p, top, total = state
        columns = slice(i * tile, (i + 1) * tile)
        acc_ref[h, :, columns] = dot(values[:, : (i + 1) * tile], p, NN)
        stat_ref[h, 0:1, columns] = top
        stat_ref[h, 1:2, columns] = total
        totals.append(total)

    in_turn(jobs, lead, score, soften, finish)

    @pl.when(too_large(totals))
    def _():
        for h in range(heads):

            @pl.loop(0, rows // tile)
            def _(i):
                columns = pl.ds(pl.multiple_of(i * tile, tile), tile)
                s = dot(k_ref[...], q_ref[columns, h * HD : (h + 1) * HD], NT) * SCALE
                at = lax.broadcasted_iota(jnp.int32, s.shape, 1) + i * tile
                s = jnp.where(lax.broadcasted_iota(jnp.int32, s.shape, 0) <= at, s, MASKED)
                top = jnp.max(s, 0, keepdims=True)
                p = jnp.exp2(s - top)
                acc_ref[h, :, columns] = dot(v_ref[...].T, p.astype(BF16), NN)
                stat_ref[h, 0:1, columns] = top
                stat_ref[h, 1:2, columns] = jnp.sum(p, 0, keepdims=True)


def anchor_kernel(pos_ref, q_ref, acc_ref, stat_ref, *refs, heads, copies):
    o_ref, k_ref, v_ref, vt_ref, sem = refs[-5:]
    copy_refs = refs[:copies]
    first = pl.program_id(0) == 0
    rows = q_ref.shape[0]
    tile = tile_of(rows)
    jobs = [(h, i) for h in range(heads) for i in range(rows // tile)]

    def fetch(act):
        for c, ref in enumerate(copy_refs):

            @pl.when(first & (pos_ref[0] == c))
            def _():
                for j, held in enumerate((k_ref, v_ref)):
                    act(pltpu.make_async_copy(ref.at[j], held, sem.at[j]))

    fetch(lambda copy: copy.start())
    fetch(lambda copy: copy.wait())

    @pl.when(pos_ref[0] < 0)
    def _():
        for h, i in jobs:
            columns = slice(i * tile, (i + 1) * tile)
            out = acc_ref[h, :, columns] / stat_ref[h, 1:2, columns]
            o_ref[columns, h * HD : (h + 1) * HD] = out.T.astype(BF16)

    @pl.when(pos_ref[0] >= 0)
    def _():
        @pl.when(first)
        def _():
            vt_ref[...] = v_ref[...].T

        keys, values = k_ref[...], vt_ref[...]
        totals = []

        def score(job):
            h, i = job
            return dot(keys, q_ref[i * tile : (i + 1) * tile, h * HD : (h + 1) * HD], NT)

        def soften(job, _, s):
            h, i = job
            columns = slice(i * tile, (i + 1) * tile)
            p = jnp.exp2(s * SCALE - stat_ref[h, 0:1, columns])
            return p.astype(BF16), stat_ref[h, 1:2, columns] + jnp.sum(p, 0, keepdims=True)

        def finish(job, state):
            h, i = job
            p, total = state
            columns = slice(i * tile, (i + 1) * tile)
            out = acc_ref[h, :, columns] + dot(values, p, NN)
            o_ref[columns, h * HD : (h + 1) * HD] = (out / total).T.astype(BF16)
            totals.append(total)

        in_turn(jobs, lambda job: None, score, soften, finish)

        @pl.when(too_large(totals))
        def _():
            for h in range(heads):

                @pl.loop(0, rows // tile)
                def _(i):
                    columns = pl.ds(pl.multiple_of(i * tile, tile), tile)
                    s = dot(k_ref[...], q_ref[columns, h * HD : (h + 1) * HD], NT) * SCALE
                    own_top = stat_ref[h, 0:1, columns]
                    top = jnp.maximum(own_top, jnp.max(s, 0, keepdims=True))
                    p = jnp.exp2(s - top)
                    factor = jnp.exp2(own_top - top)
                    total = stat_ref[h, 1:2, columns] * factor + jnp.sum(p, 0, keepdims=True)
                    out = acc_ref[h, :, columns] * factor + dot(vt_ref[...], p.astype(BF16), NN)
                    o_ref[columns, h * HD : (h + 1) * HD] = (out / total).T.astype(BF16)


def partial_kernel(lanes_ref, mine_ref, *refs, shares, kv, group):
    out_refs = refs[-shares:]
    *q_refs, k_ref, v_ref, xk_ref, xv_ref = refs[:-shares]
    share = xk_ref.shape[0]
    slots = [(ref, i) for ref in q_refs for i in range(0, ref.shape[0], share)]
    width = group * share
    mine = mine_ref[0]
    together = max(1, min(shares, 256 // width))
    row = lax.broadcasted_iota(jnp.int32, (share, together * width), 0)
    column = lax.broadcasted_iota(jnp.int32, (share, together * width), 1)

    def visible(r):
        source = (r + column // width) ^ mine
        return mine * share + row <= source * share + column % share

    packs = [(g, r) for g in range(kv) for r in range(0, shares, together)]

    def lanes(g):
        return slice(g * HD, (g + 1) * HD)

    def score(job):
        g, r = job
        q = jnp.concatenate(
            [
                ref[i : i + share, (g * group + h) * HD : (g * group + h + 1) * HD]
                for ref, i in slots[r : r + together]
                for h in range(group)
            ],
            0,
        )
        return dot(k_ref[:, lanes(g)], q, NT), dot(xk_ref[:, lanes(g)], q, NT)

    def soften(job, _, scores):
        g, r = job
        s, x = scores
        x = jnp.where(visible(r), x, MASKED)
        top = jnp.maximum(jnp.max(s, 0, keepdims=True), jnp.max(x, 0, keepdims=True)) * SCALE
        p, px = jnp.exp2(s * SCALE - top), jnp.exp2(x * SCALE - top)
        total = jnp.sum(p, 0, keepdims=True) + jnp.sum(px, 0, keepdims=True)
        return p.astype(BF16), px.astype(BF16), top, total

    def finish(job, state):
        g, r = job
        p, px, top, total = state
        acc = dot(v_ref[:, lanes(g)].T, p, NN) + dot(xv_ref[:, lanes(g)].T, px, NN)
        at = kv * width + 2 * g
        for c in range(together):
            columns = slice(c * width, (c + 1) * width)
            out_ref = out_refs[r + c]
            out_ref[g * width : (g + 1) * width, :] = acc[:, columns].T
            out_ref[at : at + 1, :width] = top[:, columns]
            out_ref[at + 1 : at + 2, :width] = total[:, columns]

    in_turn(packs, lambda job: None, score, soften, finish)


def merge_parts(part_refs, out_ref, *, kv, group):
    share = out_ref.shape[0]
    width = group * share
    for g in range(kv):
        at = kv * width + 2 * g
        tops = [ref[at : at + 1, :width] for ref in part_refs]
        overall = functools.reduce(jnp.maximum, tops)
        factors = [jnp.exp2(top - overall) for top in tops]
        summed = sum(f * ref[at + 1 : at + 2, :width] for f, ref in zip(factors, part_refs))
        out = sum(
            (f / summed).reshape(width, 1) * ref[g * width : (g + 1) * width, :]
            for f, ref in zip(factors, part_refs)
        ).astype(BF16)
        for h in range(group):
            out_ref[:, (g * group + h) * HD : (g * group + h + 1) * HD] = out[h * share : (h + 1) * share]


def merge_kernel(*refs, kv, group):
    merge_parts(refs[:-1], refs[-1], kv=kv, group=group)


def relay(blocks, last):
    half = blocks // 2
    hops, holders = [[[(0, half)]]], [half]
    while half > 1:
        half //= 2
        if last and half == 1:
            hops.append([[(z, z + 1) for z in range(0, blocks, 2)]])
            break
        hops.append([[(z, z - half) for z in holders], [(z, z + half) for z in holders]])
        holders = [z + sign * half for z in holders for sign in (-1, 1)]
    return hops


def in_hbm(*arrays):
    return [pltpu.with_memory_space_constraint(a, pltpu.HBM) for a in arrays]


def body(context_queries, context_keys, context_values, query_queries, query_keys, query_values):
    rows = context_keys.shape[0]
    kv_device = context_keys.shape[1] // HD
    heads = context_queries.shape[1] // HD
    kv = max(kv_device // lax.axis_size("rep"), 1)
    group = heads // kv
    share = query_keys.shape[0]
    blocks = lax.axis_size("ctx")
    mine = lax.axis_index("ctx")
    offset = lax.axis_index("rep") * kv if kv_device > kv else jnp.int32(0)
    params = pltpu.CompilerParams(vmem_limit_bytes=VMEM_LIMIT)
    at_once = math.gcd(group, 2)
    steps = group // at_once

    own_copy = [
        jnp.stack(
            [
                lax.dynamic_slice(a, (0, (offset + g) * HD), (rows, HD))
                for a in (context_keys, context_values)
            ]
        )
        for g in range(kv)
    ]
    hops = [relay(blocks, g == kv - 1) for g in range(kv)]
    levels = len(hops[0])
    received = [[] for _ in range(kv)]

    def chosen(g):
        copies = [pairs for some in hops[g] for pairs in some]
        return sum(
            jnp.where(mine == z, c + 1, 0) for c, pairs in enumerate(copies) for _, z in pairs
        ) - 1

    taken = [chosen(g) for g in range(kv)]

    def step(s):
        transfers = []
        for g in range(kv):
            for pairs in hops[g][s - g] if 0 <= s - g < levels else ():
                for transfer in transfers:
                    ends = [pair for _, other in transfer for pair in other]
                    if all(p[0] != e[0] and p[1] != e[1] for p in pairs for e in ends):
                        transfer.append((g, pairs))
                        break
                else:
                    transfers.append([(g, pairs)])
        pieces = {(g, pairs[0]): held(g, pairs) for transfer in transfers for g, pairs in transfer}
        for transfer in transfers:
            operand = None
            for g, pairs in transfer:
                piece = pieces[g, pairs[0]]
                sends = functools.reduce(jnp.logical_or, [mine == p[0] for p in pairs])
                operand = piece if operand is None else jnp.where(sends, piece, operand)
            got = lax.ppermute(operand, "ctx", [p for _, pairs in transfer for p in pairs])
            for g, pairs in transfer:
                received[g].append(got)

    def held(g, pairs):
        if not received[g]:
            return own_copy[g]
        piece = received[g][0]
        for c in range(1, len(received[g])):
            piece = jnp.where(taken[g] == c, received[g][c], piece)
        return jnp.where(mine == 0, own_copy[g], piece) if pairs[0][0] == 0 else piece

    def own(begin, end, queries, sums):
        return pl.pallas_call(
            functools.partial(own_kernel, heads=at_once),
            grid_spec=pltpu.PrefetchScalarGridSpec(
                num_scalar_prefetch=1,
                grid=(end - begin,),
                in_specs=[pl.BlockSpec((rows, at_once * HD), lambda j, off: (0, begin + j))]
                + [pl.BlockSpec((rows, HD), lambda j, off: (0, off[0] + (begin + j) // steps))] * 2
                + [pl.BlockSpec(memory_space=pl.ANY)] * len(sums),
                out_specs=[
                    pl.BlockSpec((at_once, HD, rows), lambda j, off: (begin + j, 0, 0)),
                    pl.BlockSpec((at_once, 2, rows), lambda j, off: (begin + j, 0, 0)),
                ],
            ),
            out_shape=[
                pltpu.HBM((heads, HD, rows), F32),
                pltpu.HBM((heads, 2, rows), F32),
            ],
            input_output_aliases={4 + i: i for i in range(len(sums))},
            compiler_params=params,
            cost_estimate=pl.CostEstimate(
                flops=4 * (end - begin) * at_once * rows * rows * HD,
                bytes_accessed=8 * rows * (end - begin) * at_once * HD,
                transcendentals=0,
            ),
            name="own",
        )(offset.reshape(1), *in_hbm(queries, context_keys, context_values, *sums))

    queries = context_queries
    slots = [query_queries] + [
        lax.ppermute(query_queries, "ctx", [(z, z ^ r) for z in range(blocks)]) for r in range(1, blocks)
    ]
    step(0)
    total = heads // at_once
    early = -(-3 * total // 4)
    sums, slots, received, queries = lax.optimization_barrier(
        (own(0, early, queries, ()), slots, received, queries)
    )
    step(1)
    payload_rows = -(-(kv * group * share + 2 * kv) // 8) * 8
    partial = pl.pallas_call(
        functools.partial(partial_kernel, shares=blocks, kv=kv, group=group),
        grid_spec=pltpu.PrefetchScalarGridSpec(
            num_scalar_prefetch=2,
            grid=(1,),
            in_specs=[pl.BlockSpec(q.shape, lambda j, at, pos: (0, 0)) for q in slots]
            + [pl.BlockSpec((rows, kv * HD), lambda j, at, pos: (0, at[0]))] * 2
            + [pl.BlockSpec((share, kv * HD), lambda j, at, pos: (0, at[0]))] * 2,
            out_specs=[pl.BlockSpec((payload_rows, HD), lambda j, at, pos: (0, 0))] * blocks,
        ),
        out_shape=[jax.ShapeDtypeStruct((payload_rows, HD), F32)] * blocks,
        compiler_params=params,
        name="partial",
    )(
        (offset // kv).reshape(1),
        mine.reshape(1),
        *slots,
        *in_hbm(context_keys, context_values),
        query_keys,
        query_values,
    )
    partial, sums, queries = lax.optimization_barrier((partial, sums, queries))
    if early < total:
        sums = own(early, total, queries, sums)
    for s in range(2, kv + levels - 1):
        sums, received, partial = lax.optimization_barrier((sums, received, partial))
        step(s)
    returned = [
        lax.ppermute(partial[r], "ctx", [(z, z ^ r) for z in range(blocks)]) for r in range(1, blocks)
    ]
    returned = [partial[0]] + returned

    context_out = None
    for g in range(kv):
        operands = [taken[g].reshape(1), *in_hbm(context_queries, *sums), *received[g]]
        in_specs = [
            pl.BlockSpec((rows, at_once * HD), lambda j, pos, g=g: (0, g * steps + j)),
            pl.BlockSpec((at_once, HD, rows), lambda j, pos, g=g: (g * steps + j, 0, 0)),
            pl.BlockSpec((at_once, 2, rows), lambda j, pos, g=g: (g * steps + j, 0, 0)),
        ] + [pl.BlockSpec(memory_space=pl.ANY)] * len(received[g])
        out_specs = [pl.BlockSpec((rows, at_once * HD), lambda j, pos, g=g: (0, g * steps + j))]
        out_shape = [jax.ShapeDtypeStruct((rows, heads * HD), BF16)]
        if g > 0:
            operands += in_hbm(context_out)
            in_specs.append(pl.BlockSpec(memory_space=pl.ANY))
        out = pl.pallas_call(
            functools.partial(
                anchor_kernel,
                heads=at_once,
                copies=len(received[g]),
            ),
            grid_spec=pltpu.PrefetchScalarGridSpec(
                num_scalar_prefetch=1,
                grid=(steps,),
                in_specs=in_specs,
                out_specs=out_specs,
                scratch_shapes=[
                    pltpu.VMEM((rows, HD), BF16),
                    pltpu.VMEM((rows, HD), BF16),
                    pltpu.VMEM((HD, rows), BF16),
                    pltpu.SemaphoreType.DMA((2,)),
                ],
            ),
            out_shape=out_shape,
            input_output_aliases={len(operands) - 1: 0} if g > 0 else {},
            compiler_params=params,
            cost_estimate=pl.CostEstimate(
                flops=4 * group * rows * rows * HD, bytes_accessed=8 * rows * group * HD, transcendentals=0
            ),
            name="anchor",
        )(*operands)
        context_out = out[0]
    context_out, returned = lax.optimization_barrier((context_out, returned))
    query_out = pl.pallas_call(
        functools.partial(merge_kernel, kv=kv, group=group),
        out_shape=jax.ShapeDtypeStruct((share, heads * HD), BF16),
        compiler_params=params,
        name="merge",
    )(*returned)
    return context_out, query_out


def solution(mesh):
    in_specs = (
        P(("groups", "ctx"), ("kvh", "rep")),
        P(("groups", "ctx"), "kvh"),
        P(("groups", "ctx"), "kvh"),
        P(("groups", "ctx"), ("kvh", "rep")),
        P(("groups", "ctx"), "kvh"),
        P(("groups", "ctx"), "kvh"),
    )
    out_specs = (P(("groups", "ctx"), ("kvh", "rep")), P(("groups", "ctx"), ("kvh", "rep")))
    return jax.shard_map(body, mesh=mesh, in_specs=in_specs, out_specs=out_specs, check_vma=False)
```
